32 devices in a mesh: section: 2 (over core), ctx: 8 (over z, x), tp: 2 (over y).
Axes of the slice: x: 2, y: 2, z: 4, core: 2. Of those that a mesh axis runs over, the one named last changes fastest.
Arguments:
- layer_input: bfloat16 [2, 1024, 1024], P(None, 'ctx'), may hold values from -6 to 6
- cotangent: bfloat16 [2, 1024, 1024], P(None, 'ctx'), may hold values from -6 to 6
- w_qkv: bfloat16 [2, 1024, 3, 1024], P('section', None, None, 'tp'), may hold values from -0.1875 to 0.1875
- b_qv: bfloat16 [2, 2, 1024], P('section', None, 'tp'), may hold values from -3 to 3
- w_out: bfloat16 [2, 1024, 1024], P('section', 'tp'), may hold values from -4 to 4
- b_out: bfloat16 [2, 1024], P('section'), may hold values from -3 to 3
- w_fc: bfloat16 [2, 1024, 4096], P('section', None, 'tp'), may hold values from -0.1875 to 0.1875
- b_fc: bfloat16 [2, 4096], P('section', 'tp'), may hold values from -3 to 3
- w_proj: bfloat16 [2, 4096, 1024], P('section', 'tp'), may hold values from -0.09375 to 0.09375
- b_proj: bfloat16 [2, 1024], P('section'), may hold values from -3 to 3
- ln_gain: float32 [2, 2, 1024], P('section'), may hold values from 0.5 to 1.5
- ln_bias: float32 [2, 2, 1024], P('section'), may hold values from -3 to 3
Outputs:
- activations: bfloat16 [2, 2, 1024, 1024], P('section', None, 'ctx')
- input_grads: float32 [2, 2, 1024, 1024], P('section', None, 'ctx')
- grad_w_qkv: float32 [2, 1024, 3, 1024], P('section', None, None, 'tp')
- grad_b_qv: float32 [2, 2, 1024], P('section', None, 'tp')
- grad_w_out: float32 [2, 1024, 1024], P('section', 'tp')
- grad_b_out: float32 [2, 1024], P('section')
- grad_w_fc: float32 [2, 1024, 4096], P('section', None, 'tp')
- grad_b_fc: float32 [2, 4096], P('section', 'tp')
- grad_w_proj: float32 [2, 4096, 1024], P('section', 'tp')
- grad_b_proj: float32 [2, 1024], P('section')
- grad_ln_gain: float32 [2, 2, 1024], P('section')
- grad_ln_bias: float32 [2, 2, 1024], P('section')
The draws below stay inside these ranges and needn't reach their ends.
All inputs are finite; a program needn't handle non-finite values.
Results may differ from the reference program's by a relative error of at most 0.028.
Values may be sent and summed in bfloat16 or wider, within the bound.
A program may use at most 192 MiB of HBM per device.

```python
import jax
import jax.numpy as jnp
from jax import lax

D = 1024
HEADS = 16
HD = 64
FF = 4096
LAYERS = 2
MB = 2
SEQ = 1024
N_TP = 2


def shard_levels(own_key, dims, pieces, least, high):
    gain = 1.0
    for position, blocks in pieces:
        heights = jax.random.uniform(jax.random.fold_in(jax.random.fold_in(own_key, 6), position), (blocks,), jnp.float32, least / len(pieces), high / len(pieces))
        gain = gain * jnp.repeat(jnp.exp(heights), dims[position] // blocks).reshape((-1,) + (1,) * (len(dims) - 1 - position))
    return gain


def centred(rng, extent, spread, limit, pieces=(), held_as=jnp.bfloat16):
    drawn = spread * jax.random.normal(rng, extent, jnp.float32)
    if pieces:
        drawn = drawn * shard_levels(rng, extent, pieces, -0.22, 0.18)
    return jnp.clip(drawn, -limit, limit).astype(held_as)


def setup_inputs(seed: int = 0) -> dict:
    streams_of = jax.random.split(jax.random.key(seed), 13)
    return {
        "layer_input": centred(streams_of[0], (MB, SEQ, D), 1.0, 6.0, ((1, 8),)),
        "cotangent": centred(streams_of[1], (MB, SEQ, D), 1.0, 6.0, ((1, 8),)),
        "w_qkv": centred(streams_of[2], (LAYERS, D, 3, D), D ** -0.5, 0.1875, ((0, 2), (3, 2))),
        "b_qv": centred(streams_of[3], (LAYERS, 2, D), 0.5, 3.0, ((0, 2), (2, 2))),
        "w_out": centred(streams_of[4], (LAYERS, D, D), (max(1, 2 * D // SEQ)) ** -0.5, 4.0, ((0, 2), (1, 2))),
        "b_out": centred(streams_of[5], (LAYERS, D), 0.5, 3.0, ((0, 2),)),
        "w_fc": centred(streams_of[6], (LAYERS, D, FF), D ** -0.5, 0.1875, ((0, 2), (2, 2))),
        "b_fc": centred(streams_of[7], (LAYERS, FF), 0.5, 3.0, ((0, 2), (1, 2))),
        "w_proj": centred(streams_of[8], (LAYERS, FF, D), FF ** -0.5, 0.09375, ((0, 2), (1, 2))),
        "b_proj": centred(streams_of[9], (LAYERS, D), 0.5, 3.0, ((0, 2),)),
        "ln_gain": jnp.clip(1.0 + 0.1 * jax.random.normal(streams_of[10], (LAYERS, 2, D), jnp.float32), 0.5, 1.5),
        "ln_bias": centred(streams_of[11], (LAYERS, 2, D), 0.2, 3.0, ((0, 2),), jnp.float32),
    }


EPS = 1e-05
GELU_C = 0.7978845608028654

def norm_forward(values, gain_vec, shift_vec):
    row_mean = lax.optimization_barrier(jnp.mean(values, axis=-1, keepdims=True))
    centered = values - row_mean
    inv_std = lax.rsqrt(lax.optimization_barrier(jnp.mean(centered * centered, axis=-1, keepdims=True)) + EPS)
    normed = centered * inv_std
    return (normed * gain_vec + shift_vec, normed, inv_std)

def norm_backward(upstream, normed, inv_std, gain_vec):
    dnormed = upstream * gain_vec
    centered_grad = dnormed - lax.optimization_barrier(jnp.mean(dnormed, axis=-1, keepdims=True)) - normed * lax.optimization_barrier(jnp.mean(dnormed * normed, axis=-1, keepdims=True))
    return (inv_std * centered_grad, lax.optimization_barrier(jnp.sum(upstream * normed, axis=0)), lax.optimization_barrier(jnp.sum(upstream, axis=0)))

def gelu_parts(pre_act):
    tanh_val = jnp.tanh(GELU_C * (pre_act + 0.044715 * pre_act * pre_act * pre_act))
    gelu_value = 0.5 * pre_act * (1.0 + tanh_val)
    gelu_slope = 0.5 * (1.0 + tanh_val) + 0.5 * pre_act * (1.0 - tanh_val * tanh_val) * GELU_C * (1.0 + 3.0 * 0.044715 * pre_act * pre_act)
    return (gelu_value, gelu_slope)

def group_sum(left_groups, right_groups):

    def accumulate(running, operands):
        portion = jnp.dot(operands[0], operands[1], preferred_element_type=jnp.float32).astype(jnp.bfloat16)
        portion = lax.optimization_barrier(portion)
        return (running + portion.astype(jnp.float32), None)
    init_state = jnp.zeros((left_groups.shape[1], right_groups.shape[2]), jnp.float32)
    summed, _ = lax.scan(accumulate, init_state, (left_groups, right_groups))
    return summed

def col_groups(values):
    return values.reshape(values.shape[0], N_TP, -1).transpose(1, 0, 2)

def row_groups(values):
    return values.reshape(N_TP, -1, values.shape[1])

def to_heads(values):
    return values.reshape(SEQ, HEADS, HD).transpose(1, 0, 2)

def from_heads(values):
    return values.transpose(1, 0, 2).reshape(SEQ, D)

def causal_mask():
    positions = jnp.arange(SEQ, dtype=jnp.int32)
    return positions[:, None] >= positions[None, :]

def attend(queries, key_rows, val_rows):
    score_scale = HD ** (-0.5)
    causal = causal_mask()

    def per_head(members):
        head_q, head_k, head_v = members
        scores = jnp.dot(head_q, head_k.T, preferred_element_type=jnp.float32) * score_scale
        weights = jnp.where(causal, jnp.exp(scores), 0.0)
        totals = lax.optimization_barrier(jnp.sum(weights, axis=-1))
        accum = jnp.dot(weights.astype(jnp.bfloat16), head_v, preferred_element_type=jnp.float32)
        return ((accum / totals[:, None]).astype(jnp.bfloat16), jnp.log(totals))
    return lax.map(per_head, (queries, key_rows, val_rows))

def attend_back(queries, key_rows, val_rows, attended, log_total, d_attended):
    score_scale = HD ** (-0.5)
    causal = causal_mask()

    def per_head(members):
        head_q, head_k, head_v, head_o, head_l, head_d = members
        scores = jnp.dot(head_q, head_k.T, preferred_element_type=jnp.float32) * score_scale
        probs = jnp.where(causal, jnp.exp(scores - head_l[:, None]), 0.0)
        row_delta = lax.optimization_barrier(jnp.sum(head_d.astype(jnp.float32) * head_o.astype(jnp.float32), axis=-1))
        d_probs = jnp.dot(head_d, head_v.T, preferred_element_type=jnp.float32)
        d_scores = (probs * (d_probs - row_delta[:, None])).astype(jnp.bfloat16)
        d_query = jnp.dot(d_scores, head_k, preferred_element_type=jnp.float32) * score_scale
        d_key = jnp.dot(d_scores.T, head_q, preferred_element_type=jnp.float32) * score_scale
        d_val = jnp.dot(probs.astype(jnp.bfloat16).T, head_d, preferred_element_type=jnp.float32)
        return (d_query, d_key, d_val)
    return lax.map(per_head, (queries, key_rows, val_rows, attended, log_total, d_attended))

def layer_forward(layer_in, weights_set):
    w_qkv, b_qv, w_out, b_out, w_fc, b_fc, w_proj, b_proj, ln_gain, ln_bias = weights_set
    layer_f32 = layer_in.astype(jnp.float32)
    first_norm, normed_a, inv_a = norm_forward(layer_f32, ln_gain[0], ln_bias[0])
    first_bf = first_norm.astype(jnp.bfloat16)
    joined = jnp.dot(first_bf, w_qkv.reshape(D, 3 * D), preferred_element_type=jnp.float32).reshape(SEQ, 3, D)
    queries = (joined[:, 0] + b_qv[0].astype(jnp.float32)).astype(jnp.bfloat16)
    key_rows = joined[:, 1].astype(jnp.bfloat16)
    val_rows = (joined[:, 2] + b_qv[1].astype(jnp.float32)).astype(jnp.bfloat16)
    head_out, log_total = attend(to_heads(queries), to_heads(key_rows), to_heads(val_rows))
    attended = from_heads(head_out)
    attn_mixed = group_sum(col_groups(attended), row_groups(w_out))
    hidden_in = layer_f32 + attn_mixed + b_out.astype(jnp.float32)
    second_norm, normed_b, inv_b = norm_forward(hidden_in, ln_gain[1], ln_bias[1])
    second_bf = second_norm.astype(jnp.bfloat16)
    pre_act = jnp.dot(second_bf, w_fc, preferred_element_type=jnp.float32) + b_fc.astype(jnp.float32)
    gelu_value, gelu_slope = gelu_parts(pre_act)
    act_bf = gelu_value.astype(jnp.bfloat16)
    result = hidden_in + group_sum(col_groups(act_bf), row_groups(w_proj)) + b_proj.astype(jnp.float32)
    saved = (normed_a, inv_a, first_bf, queries, key_rows, val_rows, head_out, log_total, attended, normed_b, inv_b, second_bf, act_bf, gelu_slope)
    return (result.astype(jnp.bfloat16), saved)

def layer_backward(upstream, saved, weights_set):
    w_qkv, b_qv, w_out, b_out, w_fc, b_fc, w_proj, b_proj, ln_gain, ln_bias = weights_set
    normed_a, inv_a, first_bf, queries, key_rows, val_rows, head_out, log_total, attended, normed_b, inv_b, second_bf, act_bf, gelu_slope = saved
    up_bf = upstream.astype(jnp.bfloat16)
    grad_b_proj = lax.optimization_barrier(jnp.sum(upstream, axis=0))
    grad_w_proj = jnp.dot(act_bf.T, up_bf, preferred_element_type=jnp.float32)
    d_pre = jnp.dot(up_bf, w_proj.T, preferred_element_type=jnp.float32) * gelu_slope
    d_pre_bf = d_pre.astype(jnp.bfloat16)
    grad_b_fc = lax.optimization_barrier(jnp.sum(d_pre, axis=0))
    grad_w_fc = jnp.dot(second_bf.T, d_pre_bf, preferred_element_type=jnp.float32)
    d_second = group_sum(col_groups(d_pre_bf), row_groups(w_fc.T))
    d_hidden_ln, gain_b, shift_b = norm_backward(d_second, normed_b, inv_b, ln_gain[1])
    d_hidden = upstream + d_hidden_ln
    grad_b_out = lax.optimization_barrier(jnp.sum(d_hidden, axis=0))
    hidden_bf = d_hidden.astype(jnp.bfloat16)
    grad_w_out = jnp.dot(attended.T, hidden_bf, preferred_element_type=jnp.float32)
    d_attended = jnp.dot(hidden_bf, w_out.T, preferred_element_type=jnp.float32).astype(jnp.bfloat16)
    d_query, d_key, d_val = attend_back(to_heads(queries), to_heads(key_rows), to_heads(val_rows), head_out, log_total, to_heads(d_attended))
    d_query = from_heads(d_query)
    d_key = from_heads(d_key)
    d_val = from_heads(d_val)
    grad_b_qv = jnp.stack([lax.optimization_barrier(jnp.sum(d_query, axis=0)), lax.optimization_barrier(jnp.sum(d_val, axis=0))])
    d_joined = jnp.stack([d_query, d_key, d_val], axis=1).astype(jnp.bfloat16)
    grad_w_qkv = jnp.dot(first_bf.T, d_joined.reshape(SEQ, 3 * D), preferred_element_type=jnp.float32).reshape(D, 3, D)
    left_groups = d_joined.reshape(SEQ, 3, N_TP, D // N_TP).transpose(2, 0, 1, 3).reshape(N_TP, SEQ, 3 * (D // N_TP))
    right_groups = w_qkv.reshape(D, 3, N_TP, D // N_TP).transpose(2, 1, 3, 0).reshape(N_TP, 3 * (D // N_TP), D)
    d_first = group_sum(left_groups, right_groups)
    d_in_ln, gain_a, shift_a = norm_backward(d_first, normed_a, inv_a, ln_gain[0])
    d_input = d_hidden + d_in_ln
    grads = (grad_w_qkv, grad_b_qv, grad_w_out, grad_b_out, grad_w_fc, grad_b_fc, grad_w_proj, grad_b_proj, jnp.stack([gain_a, gain_b]), jnp.stack([shift_a, shift_b]))
    return (d_input, grads)

def reference(layer_input, cotangent, w_qkv, b_qv, w_out, b_out, w_fc, b_fc, w_proj, b_proj, ln_gain, ln_bias):
    layer_sets = []
    for layer_index in range(LAYERS):
        layer_sets.append((w_qkv[layer_index], b_qv[layer_index], w_out[layer_index], b_out[layer_index], w_fc[layer_index], b_fc[layer_index], w_proj[layer_index], b_proj[layer_index], ln_gain[layer_index], ln_bias[layer_index]))
    outputs_all = [[] for layer_index in range(LAYERS)]
    saved_all = [[] for layer_index in range(LAYERS)]
    for batch_index in range(MB):
        layer_in = layer_input[batch_index]
        for layer_index in range(LAYERS):
            result, saved = layer_forward(layer_in, layer_sets[layer_index])
            outputs_all[layer_index].append(result)
            saved_all[layer_index].append(saved)
            layer_in = result
    grads_all = [None for layer_index in range(LAYERS)]
    input_grads_all = [[] for layer_index in range(LAYERS)]
    for batch_index in range(MB):
        upstream = cotangent[batch_index].astype(jnp.float32)
        for layer_index in reversed(range(LAYERS)):
            d_input, grads = layer_backward(upstream, saved_all[layer_index][batch_index], layer_sets[layer_index])
            if grads_all[layer_index] is None:
                grads_all[layer_index] = grads
            else:
                grads_all[layer_index] = jax.tree.map(jnp.add, grads_all[layer_index], grads)
            input_grads_all[layer_index].append(d_input)
            upstream = d_input
    activations = jnp.stack([jnp.stack(outputs_all[layer_index]) for layer_index in range(LAYERS)])
    input_grads = jnp.stack([jnp.stack(input_grads_all[layer_index]) for layer_index in range(LAYERS)])
    stacked = [jnp.stack([grads_all[layer_index][member] for layer_index in range(LAYERS)]) for member in range(10)]
    return (activations, input_grads, stacked[0], stacked[1], stacked[2], stacked[3], stacked[4], stacked[5], stacked[6], stacked[7], stacked[8], stacked[9])
```

```python
import functools

import jax
import jax.numpy as jnp
from jax import lax
from jax.experimental import pallas as pl
from jax.experimental.pallas import tpu as pltpu
from jax.sharding import PartitionSpec as P

HD = 64
EPS = 1e-05
GELU_C = 0.7978845608028654
F32 = jnp.float32
BF16 = jnp.bfloat16


def dot(lhs, rhs, lhs_dim, rhs_dim):
    return lax.dot_general(
        lhs, rhs, (((lhs_dim,), (rhs_dim,)), ((), ())), preferred_element_type=F32
    )


def norm_forward(values, gain_vec, shift_vec):
    row_mean = jnp.mean(values, axis=-1, keepdims=True)
    centered = values - row_mean
    inv_std = lax.rsqrt(jnp.mean(centered * centered, axis=-1, keepdims=True) + EPS)
    normed = centered * inv_std
    return (normed * gain_vec + shift_vec, normed, inv_std)


def norm_backward(upstream, normed, inv_std, gain_vec):
    dnormed = upstream * gain_vec
    centered_grad = (
        dnormed
        - jnp.mean(dnormed, axis=-1, keepdims=True)
        - normed * jnp.mean(dnormed * normed, axis=-1, keepdims=True)
    )
    return (inv_std * centered_grad, jnp.sum(upstream * normed, axis=0), jnp.sum(upstream, axis=0))


def gelu_parts(pre_act):
    tanh_val = jnp.tanh(GELU_C * (pre_act + 0.044715 * pre_act * pre_act * pre_act))
    gelu_value = 0.5 * pre_act * (1.0 + tanh_val)
    gelu_slope = 0.5 * (1.0 + tanh_val) + 0.5 * pre_act * (1.0 - tanh_val * tanh_val) * GELU_C * (
        1.0 + 3.0 * 0.044715 * pre_act * pre_act
    )
    return (gelu_value, gelu_slope)


def swap(value):
    return lax.ppermute(value, "section", [(0, 1), (1, 0)])


def tp_sum(part):
    part = part.astype(BF16)
    if lax.axis_size("tp") == 2:
        other = lax.ppermute(part, "tp", [(0, 1), (1, 0)])
        return part.astype(F32) + other.astype(F32)
    return lax.psum(part, "tp").astype(F32)


def a2a_kernel(n, x_ref, o_ref, send_sem, recv_sem, own_sem):
    me = lax.axis_index("ctx")
    barrier = pltpu.get_barrier_semaphore()
    for step in range(1, n):
        pl.semaphore_signal(
            barrier,
            inc=1,
            device_id={"ctx": lax.rem(me + step, n)},
            device_id_type=pl.DeviceIdType.MESH,
        )
    pl.semaphore_wait(barrier, n - 1)
    copies = []
    for step in range(1, n):
        peer = lax.rem(me + step, n)
        copy = pltpu.make_async_remote_copy(
            src_ref=x_ref.at[peer],
            dst_ref=o_ref.at[me],
            send_sem=send_sem.at[step],
            recv_sem=recv_sem.at[step],
            device_id={"ctx": peer},
            device_id_type=pl.DeviceIdType.MESH,
        )
        copy.start()
        copies.append(copy)
    own = pltpu.make_async_copy(x_ref.at[me], o_ref.at[me], own_sem)
    own.start()
    own.wait()
    for copy in copies:
        copy.wait()


def all_to_all(value, collective_id):
    n = value.shape[0]
    return pl.pallas_call(
        functools.partial(a2a_kernel, n),
        out_shape=jax.ShapeDtypeStruct(value.shape, value.dtype),
        in_specs=[pl.BlockSpec(memory_space=pltpu.VMEM)],
        out_specs=pl.BlockSpec(memory_space=pltpu.VMEM),
        scratch_shapes=[
            pltpu.SemaphoreType.DMA((n,)),
            pltpu.SemaphoreType.DMA((n,)),
            pltpu.SemaphoreType.DMA,
        ],
        compiler_params=pltpu.CompilerParams(collective_id=collective_id, has_side_effects=True),
        name="a2a",
    )(value)


def to_heads(value, collective_id):
    parts, cols, rows = value.shape
    n = lax.axis_size("ctx")
    sent = value.reshape(parts, n, cols // n, rows).transpose(1, 0, 2, 3)
    got = all_to_all(sent.reshape(n, parts * cols // n, rows), collective_id)
    got = got.reshape(n, parts, cols // n, rows).transpose(1, 2, 0, 3)
    return got.reshape(parts, cols // n // HD, HD, n * rows)


def to_tokens(value, collective_id):
    parts, heads, _, total = value.shape
    n = lax.axis_size("ctx")
    rows = total // n
    sent = value.reshape(parts, heads * HD, n, rows).transpose(2, 0, 1, 3)
    got = all_to_all(sent.reshape(n, parts * heads * HD, rows), collective_id)
    got = got.reshape(n, parts, heads * HD, rows).transpose(1, 0, 2, 3)
    return got.reshape(parts, n * heads * HD, rows)


def scores_of(queries, keys):
    return jnp.einsum("hdk,hdq->hkq", keys, queries, preferred_element_type=F32) * HD ** (-0.5)


def causal_of(query_pos, key_count):
    return (jnp.arange(key_count, dtype=jnp.int32)[:, None] <= query_pos[None, :])[None]


def attend(queries, keys, vals, query_pos):
    weights = jnp.where(
        causal_of(query_pos, keys.shape[2]), jnp.exp(scores_of(queries, keys)), 0.0
    )
    totals = jnp.sum(weights, axis=1)
    out = jnp.einsum("hdk,hkq->hdq", vals, weights.astype(BF16), preferred_element_type=F32)
    return (out / totals[:, None, :]).astype(BF16), jnp.log(totals)


def attend_backward(queries, keys, vals, attended, log_total, d_out, query_pos):
    probs = jnp.where(
        causal_of(query_pos, keys.shape[2]),
        jnp.exp(scores_of(queries, keys) - log_total[:, None, :]),
        0.0,
    )
    delta = jnp.sum(d_out.astype(F32) * attended.astype(F32), axis=1)
    d_probs = jnp.einsum("hdk,hdq->hkq", vals, d_out, preferred_element_type=F32)
    d_scores = (probs * (d_probs - delta[:, None, :])).astype(BF16)
    scale = HD ** (-0.5)
    d_query = jnp.einsum("hdk,hkq->hdq", keys, d_scores, preferred_element_type=F32) * scale
    d_key = jnp.einsum("hdq,hkq->hdk", queries, d_scores, preferred_element_type=F32) * scale
    d_val = jnp.einsum("hdq,hkq->hdk", d_out, probs.astype(BF16), preferred_element_type=F32)
    return d_query, d_key, d_val


def attention_forward(joined):
    _, cols, rows = joined.shape
    n = lax.axis_size("ctx")
    heads = cols // HD
    if heads % n == 0:
        mine = to_heads(joined, 0)
        pos = jnp.arange(n * rows, dtype=jnp.int32)
        out, log_total = attend(mine[0], mine[1], mine[2], pos)
        local = to_tokens(out[None], 1)[0]
        return local, (mine[0], mine[1], mine[2], out, log_total)
    split = joined.reshape(3, heads, HD, rows)
    gathered = lax.all_gather(split[1:], "ctx", axis=3, tiled=True)
    pos = lax.axis_index("ctx") * rows + jnp.arange(rows, dtype=jnp.int32)
    out, log_total = attend(split[0], gathered[0], gathered[1], pos)
    return out.reshape(cols, rows), (split[0], gathered[0], gathered[1], out, log_total)


def attention_backward(saved, d_attended):
    cols, rows = d_attended.shape
    n = lax.axis_size("ctx")
    heads = cols // HD
    if heads % n == 0:
        pos = jnp.arange(n * rows, dtype=jnp.int32)
        d_out = to_heads(d_attended[None], 1)[0]
        parts = attend_backward(*saved, d_out, pos)
        return to_tokens(jnp.stack([part.astype(BF16) for part in parts]), 0)
    pos = lax.axis_index("ctx") * rows + jnp.arange(rows, dtype=jnp.int32)
    d_query, d_key, d_val = attend_backward(*saved, d_attended.reshape(heads, HD, rows), pos)
    d_kv = lax.psum_scatter(
        jnp.stack([d_key, d_val]).astype(BF16), "ctx", scatter_dimension=3, tiled=True
    )
    return jnp.concatenate([d_query.astype(BF16)[None], d_kv]).reshape(3, cols, rows)


def layer_forward(layer_in, weights, vecs):
    w_qkv, w_out, w_fc, w_proj = weights
    b_q, b_v, b_out, b_fc, b_proj, gain_a, gain_b, shift_a, shift_b = vecs
    rows, width = layer_in.shape
    cols = w_out.shape[0]
    layer_f32 = layer_in.astype(F32)
    first, normed_a, inv_a = norm_forward(layer_f32, gain_a, shift_a)
    first = first.astype(BF16)
    joined = dot(w_qkv, first, 0, 1).reshape(3, cols, rows)
    bias = jnp.stack([b_q, jnp.zeros_like(b_q), b_v])[:, :, None]
    attended, attn_saved = attention_forward((joined + bias).astype(BF16))
    hidden = layer_f32 + tp_sum(dot(attended, w_out, 0, 0)) + b_out
    second, normed_b, inv_b = norm_forward(hidden, gain_b, shift_b)
    second = second.astype(BF16)
    act, slope = gelu_parts(dot(second, w_fc, 1, 0) + b_fc)
    act = act.astype(BF16)
    result = (hidden + tp_sum(dot(act, w_proj, 1, 0)) + b_proj).astype(BF16)
    return result, (normed_a, inv_a, first, attended, attn_saved, normed_b, inv_b, second, act, slope)


def cross(later, split, whole):
    half = split.shape[1] // 2
    low, high = split[:, :half], split[:, half:]
    sent = jnp.concatenate([jnp.where(later, low, high), whole], axis=1)
    got = swap(sent)
    both = jnp.concatenate([jnp.concatenate([jnp.where(later, high, low), whole], axis=1), got])
    return both[:, :half], both[:, half:]


def half_grad(later, split, whole):
    mine, other = cross(later, split, whole)
    return dot(mine, other, 0, 0).astype(BF16)


def ctx_sums(queue, values):
    if queue:
        values, queue[-1] = lax.optimization_barrier((values, queue[-1]))
    queue.append([lax.psum(value, "ctx") for value in values])


def layer_backward(upstream, saved, weights, vecs, later, queue):
    w_qkv, w_out, w_fc, w_proj = weights
    _, _, _, _, _, gain_a, gain_b, _, _ = vecs
    normed_a, inv_a, first, attended, attn_saved, normed_b, inv_b, second, act, slope = saved
    up_bf = upstream.astype(BF16)
    d_pre = dot(up_bf, w_proj, 1, 1) * slope
    d_pre_bf = d_pre.astype(BF16)
    d_second = tp_sum(dot(d_pre_bf, w_fc, 1, 1))
    g_proj = half_grad(later, act, up_bf)
    g_fc = half_grad(later, second, d_pre_bf)
    ctx_sums(queue, [g_proj, g_fc])
    d_hidden_ln, gain_b_grad, shift_b_grad = norm_backward(d_second, normed_b, inv_b, gain_b)
    d_hidden = upstream + d_hidden_ln
    hidden_bf = d_hidden.astype(BF16)
    d_attended = dot(w_out, hidden_bf, 1, 1).astype(BF16)
    g_out = half_grad(later, attended.T, hidden_bf)
    d_joined = attention_backward(attn_saved, d_attended)
    _, cols, rows = d_joined.shape
    flat = d_joined.reshape(3 * cols, rows)
    d_first = tp_sum(dot(flat, w_qkv, 0, 1))
    g_qkv = half_grad(later, first, flat.T)
    d_in_ln, gain_a_grad, shift_a_grad = norm_backward(d_first, normed_a, inv_a, gain_a)
    bias_grads = jnp.sum(d_joined.astype(F32), axis=2)
    small = jnp.concatenate(
        [
            bias_grads[0],
            bias_grads[2],
            jnp.sum(d_hidden, axis=0),
            jnp.sum(d_pre, axis=0),
            jnp.sum(upstream, axis=0),
            gain_a_grad,
            gain_b_grad,
            shift_a_grad,
            shift_b_grad,
        ]
    )
    return d_hidden + d_in_ln, [g_out, g_qkv], small


def body(
    layer_input, cotangent, w_qkv, b_qv, w_out, b_out, w_fc, b_fc, w_proj, b_proj, ln_gain, ln_bias
):
    later = lax.axis_index("section") == 1
    width = layer_input.shape[2]
    cols = w_out.shape[1]

    def both_layers(own):
        other = swap(own)
        return jnp.where(later, other, own), jnp.where(later, own, other)

    vec_parts = [
        b_qv[0, 0], b_qv[0, 1], b_out[0], b_fc[0], b_proj[0],
        ln_gain[0, 0], ln_gain[0, 1], ln_bias[0, 0], ln_bias[0, 1],
    ]
    bounds = []
    for part in vec_parts:
        bounds.append((bounds[-1] if bounds else 0) + part.shape[0])
    vec_pair = both_layers(jnp.concatenate([part.astype(F32) for part in vec_parts]))
    vecs = [jnp.split(vec, bounds[:-1]) for vec in vec_pair]
    mats = [
        both_layers(mat)
        for mat in (w_qkv[0].reshape(width, 3 * cols), w_out[0], w_fc[0], w_proj[0])
    ]
    weights = [[pair[layer] for pair in mats] for layer in range(2)]

    start = jnp.where(later, layer_input[1], layer_input[0])
    act_0, saved_0 = layer_forward(start, weights[0], vecs[0])
    act_1, saved_1 = layer_forward(act_0, weights[1], vecs[1])
    got_act = swap(jnp.where(later, act_0, act_1))
    activations = jnp.stack([jnp.where(later, got_act, act_0), jnp.where(later, act_1, got_act)])

    upstream = jnp.where(later, cotangent[1], cotangent[0]).astype(F32)
    queue = []
    d_1, attn_1, small_1 = layer_backward(upstream, saved_1, weights[1], vecs[1], later, queue)
    ctx_sums(queue, attn_1)
    d_0, attn_0, small_0 = layer_backward(d_1, saved_0, weights[0], vecs[0], later, queue)
    small = jnp.where(later, small_1, small_0) + swap(jnp.where(later, small_0, small_1))
    ctx_sums(queue, attn_0 + [small])
    small = queue[3].pop()
    sums_1, sums_0 = queue[0] + queue[1], queue[2] + queue[3]
    up_1 = [lax.ppermute(half, "section", [(0, 1)]) for half in sums_1]
    down_0 = [lax.ppermute(half, "section", [(1, 0)]) for half in sums_0]

    got_grad = swap(jnp.where(later, d_0, d_1).astype(BF16)).astype(F32)
    input_grads = jnp.stack([jnp.where(later, got_grad, d_0), jnp.where(later, d_1, got_grad)])

    def joined_halves(own_0, own_1, got_0, got_1):
        low = jnp.where(later, got_1, own_0)
        high = jnp.where(later, own_1, got_0)
        return jnp.concatenate([low, high]).astype(F32)

    g_proj, g_fc, g_out, g_qkv = [
        joined_halves(*group) for group in zip(sums_0, sums_1, down_0, up_1)
    ]
    small = jnp.split(small, bounds[:-1])
    return (
        activations[None],
        input_grads[None],
        g_qkv.reshape(1, width, 3, cols),
        jnp.stack([small[0], small[1]])[None],
        g_out[None],
        small[2][None],
        g_fc[None],
        small[3][None],
        g_proj[None],
        small[4][None],
        jnp.stack([small[5], small[6]])[None],
        jnp.stack([small[7], small[8]])[None],
    )


def solution(mesh):
    placed = (
        P(None, "ctx", None),
        P(None, "ctx", None),
        P("section", None, None, "tp"),
        P("section", None, "tp"),
        P("section", "tp", None),
        P("section", None),
        P("section", None, "tp"),
        P("section", "tp"),
        P("section", "tp", None),
        P("section", None),
        P("section", None, None),
        P("section", None, None),
    )
    return jax.shard_map(
        body,
        mesh=mesh,
        in_specs=placed,
        out_specs=(
            P("section", None, "ctx", None),
            P("section", None, "ctx", None),
            P("section", None, None, "tp"),
            P("section", None, "tp"),
            P("section", "tp", None),
            P("section", None),
            P("section", None, "tp"),
            P("section", "tp"),
            P("section", "tp", None),
            P("section", None),
            P("section", None, None),
            P("section", None, None),
        ),
        check_vma=False,
    )
```

```python
import functools

import jax
import jax.numpy as jnp
from jax import lax
from jax.experimental import pallas as pl
from jax.experimental.pallas import tpu as pltpu
from jax.sharding import PartitionSpec as P

HD = 64
EPS = 1e-05
GELU_C = 0.7978845608028654
F32 = jnp.float32
BF16 = jnp.bfloat16


def dot(lhs, rhs, lhs_dim, rhs_dim):
    return lax.dot_general(
        lhs, rhs, (((lhs_dim,), (rhs_dim,)), ((), ())), preferred_element_type=F32
    )


def norm_forward(values, gain_vec, shift_vec):
    row_mean = jnp.mean(values, axis=-1, keepdims=True)
    centered = values - row_mean
    inv_std = lax.rsqrt(jnp.mean(centered * centered, axis=-1, keepdims=True) + EPS)
    normed = centered * inv_std
    return (normed * gain_vec + shift_vec, normed, inv_std)


def norm_backward(upstream, normed, inv_std, gain_vec):
    dnormed = upstream * gain_vec
    centered_grad = (
        dnormed
        - jnp.mean(dnormed, axis=-1, keepdims=True)
        - normed * jnp.mean(dnormed * normed, axis=-1, keepdims=True)
    )
    return (inv_std * centered_grad, jnp.sum(upstream * normed, axis=0), jnp.sum(upstream, axis=0))


def gelu_parts(pre_act):
    tanh_val = jnp.tanh(GELU_C * (pre_act + 0.044715 * pre_act * pre_act * pre_act))
    gelu_value = 0.5 * pre_act * (1.0 + tanh_val)
    gelu_slope = 0.5 * (1.0 + tanh_val) + 0.5 * pre_act * (1.0 - tanh_val * tanh_val) * GELU_C * (
        1.0 + 3.0 * 0.044715 * pre_act * pre_act
    )
    return (gelu_value, gelu_slope)


def swap(value):
    return lax.ppermute(value, "section", [(0, 1), (1, 0)])


def tp_sum(part):
    part = part.astype(BF16)
    if lax.axis_size("tp") == 2:
        other = lax.ppermute(part, "tp", [(0, 1), (1, 0)])
        return part.astype(F32) + other.astype(F32)
    return lax.psum(part, "tp").astype(F32)


def a2a_kernel(n, x_ref, o_ref, send_sem, recv_sem, own_sem):
    me = lax.axis_index("ctx")
    barrier = pltpu.get_barrier_semaphore()
    for step in range(1, n):
        pl.semaphore_signal(
            barrier,
            inc=1,
            device_id={"ctx": lax.rem(me + step, n)},
            device_id_type=pl.DeviceIdType.MESH,
        )
    pl.semaphore_wait(barrier, n - 1)
    copies = []
    for step in range(1, n):
        peer = lax.rem(me + step, n)
        copy = pltpu.make_async_remote_copy(
            src_ref=x_ref.at[peer],
            dst_ref=o_ref.at[me],
            send_sem=send_sem.at[step],
            recv_sem=recv_sem.at[step],
            device_id={"ctx": peer},
            device_id_type=pl.DeviceIdType.MESH,
        )
        copy.start()
        copies.append(copy)
    own = pltpu.make_async_copy(x_ref.at[me], o_ref.at[me], own_sem)
    own.start()
    own.wait()
    for copy in copies:
        copy.wait()


def all_to_all(value, collective_id):
    n = value.shape[0]
    return pl.pallas_call(
        functools.partial(a2a_kernel, n),
        out_shape=jax.ShapeDtypeStruct(value.shape, value.dtype),
        in_specs=[pl.BlockSpec(memory_space=pltpu.VMEM)],
        out_specs=pl.BlockSpec(memory_space=pltpu.VMEM),
        scratch_shapes=[
            pltpu.SemaphoreType.DMA((n,)),
            pltpu.SemaphoreType.DMA((n,)),
            pltpu.SemaphoreType.DMA,
        ],
        compiler_params=pltpu.CompilerParams(collective_id=collective_id, has_side_effects=True),
        name="a2a",
    )(value)


def to_heads(value, collective_id):
    parts, cols, rows = value.shape
    n = lax.axis_size("ctx")
    sent = value.reshape(parts, n, cols // n, rows).transpose(1, 0, 2, 3)
    got = all_to_all(sent.reshape(n, parts * cols // n, rows), collective_id)
    got = got.reshape(n, parts, cols // n, rows).transpose(1, 2, 0, 3)
    return got.reshape(parts, cols // n // HD, HD, n * rows)


def to_tokens(value, collective_id):
    parts, heads, _, total = value.shape
    n = lax.axis_size("ctx")
    rows = total // n
    sent = value.reshape(parts, heads * HD, n, rows).transpose(2, 0, 1, 3)
    got = all_to_all(sent.reshape(n, parts * heads * HD, rows), collective_id)
    got = got.reshape(n, parts, heads * HD, rows).transpose(1, 0, 2, 3)
    return got.reshape(parts, n * heads * HD, rows)


def scores_of(queries, keys):
    return jnp.einsum("hdk,hdq->hkq", keys, queries, preferred_element_type=F32) * HD ** (-0.5)


def causal_of(query_pos, key_count):
    return (jnp.arange(key_count, dtype=jnp.int32)[:, None] <= query_pos[None, :])[None]


def attend(queries, keys, vals, query_pos):
    weights = jnp.where(
        causal_of(query_pos, keys.shape[2]), jnp.exp(scores_of(queries, keys)), 0.0
    )
    totals = jnp.sum(weights, axis=1)
    out = jnp.einsum("hdk,hkq->hdq", vals, weights.astype(BF16), preferred_element_type=F32)
    return (out / totals[:, None, :]).astype(BF16), jnp.log(totals)


def attend_backward(queries, keys, vals, attended, log_total, d_out, query_pos):
    probs = jnp.where(
        causal_of(query_pos, keys.shape[2]),
        jnp.exp(scores_of(queries, keys) - log_total[:, None, :]),
        0.0,
    )
    delta = jnp.sum(d_out.astype(F32) * attended.astype(F32), axis=1)
    d_probs = jnp.einsum("hdk,hdq->hkq", vals, d_out, preferred_element_type=F32)
    d_scores = (probs * (d_probs - delta[:, None, :])).astype(BF16)
    scale = HD ** (-0.5)
    d_query = jnp.einsum("hdk,hkq->hdq", keys, d_scores, preferred_element_type=F32) * scale
    d_key = jnp.einsum("hdq,hkq->hdk", queries, d_scores, preferred_element_type=F32) * scale
    d_val = jnp.einsum("hdq,hkq->hdk", d_out, probs.astype(BF16), preferred_element_type=F32)
    return d_query, d_key, d_val


def attention_forward(joined):
    _, cols, rows = joined.shape
    n = lax.axis_size("ctx")
    heads = cols // HD
    if heads % n == 0:
        mine = to_heads(joined, 0)
        pos = jnp.arange(n * rows, dtype=jnp.int32)
        out, log_total = attend(mine[0], mine[1], mine[2], pos)
        local = to_tokens(out[None], 1)[0]
        return local, (mine[0], mine[1], mine[2], out, log_total)
    split = joined.reshape(3, heads, HD, rows)
    gathered = lax.all_gather(split[1:], "ctx", axis=3, tiled=True)
    pos = lax.axis_index("ctx") * rows + jnp.arange(rows, dtype=jnp.int32)
    out, log_total = attend(split[0], gathered[0], gathered[1], pos)
    return out.reshape(cols, rows), (split[0], gathered[0], gathered[1], out, log_total)


def attention_backward(saved, d_attended):
    cols, rows = d_attended.shape
    n = lax.axis_size("ctx")
    heads = cols // HD
    if heads % n == 0:
        pos = jnp.arange(n * rows, dtype=jnp.int32)
        d_out = to_heads(d_attended[None], 1)[0]
        parts = attend_backward(*saved, d_out, pos)
        return to_tokens(jnp.stack([part.astype(BF16) for part in parts]), 0)
    pos = lax.axis_index("ctx") * rows + jnp.arange(rows, dtype=jnp.int32)
    d_query, d_key, d_val = attend_backward(*saved, d_attended.reshape(heads, HD, rows), pos)
    d_kv = lax.psum_scatter(
        jnp.stack([d_key, d_val]).astype(BF16), "ctx", scatter_dimension=3, tiled=True
    )
    return jnp.concatenate([d_query.astype(BF16)[None], d_kv]).reshape(3, cols, rows)


def layer_forward(layer_in, weights, vecs):
    w_qkv, w_out, w_fc, w_proj = weights
    b_q, b_v, b_out, b_fc, b_proj, gain_a, gain_b, shift_a, shift_b = vecs
    rows, width = layer_in.shape
    cols = w_out.shape[0]
    layer_f32 = layer_in.astype(F32)
    first, normed_a, inv_a = norm_forward(layer_f32, gain_a, shift_a)
    first = first.astype(BF16)
    joined = dot(w_qkv, first, 0, 1).reshape(3, cols, rows)
    bias = jnp.stack([b_q, jnp.zeros_like(b_q), b_v])[:, :, None]
    attended, attn_saved = attention_forward((joined + bias).astype(BF16))
    hidden = layer_f32 + tp_sum(dot(attended, w_out, 0, 0)) + b_out
    second, normed_b, inv_b = norm_forward(hidden, gain_b, shift_b)
    second = second.astype(BF16)
    act, slope = gelu_parts(dot(second, w_fc, 1, 0) + b_fc)
    act = act.astype(BF16)
    result = (hidden + tp_sum(dot(act, w_proj, 1, 0)) + b_proj).astype(BF16)
    return result, (normed_a, inv_a, first, attended, attn_saved, normed_b, inv_b, second, act, slope)


def cross(later, split, whole):
    half = split.shape[1] // 2
    low, high = split[:, :half], split[:, half:]
    sent = jnp.concatenate([jnp.where(later, low, high), whole], axis=1)
    got = swap(sent)
    both = jnp.concatenate([jnp.concatenate([jnp.where(later, high, low), whole], axis=1), got])
    return both[:, :half], both[:, half:]


def half_grad(later, split, whole):
    mine, other = cross(later, split, whole)
    return dot(mine, other, 0, 0)


def tree_sum(value, order):
    n = lax.axis_size("ctx")
    me = lax.axis_index("ctx")

    def partner(part, bit):
        return lax.ppermute(part, "ctx", [(source, source ^ bit) for source in range(n)])

    for bit in order:
        upper = lax.rem(me // bit, 2) == 1
        half = value.shape[0] // 2
        low, high = value[:half], value[half:]
        got = partner(jnp.where(upper, low, high).astype(BF16), bit)
        value = jnp.where(upper, high, low) + got.astype(F32)
    value = value.astype(BF16)
    for bit in order[::-1]:
        upper = lax.rem(me // bit, 2) == 1
        got = partner(value, bit)
        value = jnp.where(
            upper, jnp.concatenate([got, value]), jnp.concatenate([value, got])
        )
    return value


def attn_sums(g_out, g_qkv):
    n = lax.axis_size("ctx")
    rows, width = g_qkv.shape
    fold = rows // g_out.shape[0]
    if n & (n - 1) or rows % (2 * n) or rows % g_out.shape[0] or g_out.shape[1] % fold:
        return [lax.psum(g_out.astype(BF16), "ctx"), lax.psum(g_qkv.astype(BF16), "ctx")]
    bits = [1 << power for power in range(n.bit_length() - 1)]
    folded = jnp.concatenate(jnp.split(g_out, fold, axis=1), axis=0)
    both = jnp.concatenate([g_qkv, folded], axis=1)
    half = rows // 2
    total = jnp.concatenate(
        [tree_sum(both[:half], bits), tree_sum(both[half:], bits[1:] + bits[:1])]
    )
    out = jnp.concatenate(jnp.split(total[:, width:], fold, axis=0), axis=1)
    return [out, total[:, :width]]


def layer_backward(upstream, saved, weights, vecs, later):
    w_qkv, w_out, w_fc, w_proj = weights
    _, _, _, _, _, gain_a, gain_b, _, _ = vecs
    normed_a, inv_a, first, attended, attn_saved, normed_b, inv_b, second, act, slope = saved
    up_bf = upstream.astype(BF16)
    d_pre = dot(up_bf, w_proj, 1, 1) * slope
    d_pre_bf = d_pre.astype(BF16)
    d_second = tp_sum(dot(d_pre_bf, w_fc, 1, 1))
    g_proj = half_grad(later, act, up_bf).astype(BF16)
    g_fc = half_grad(later, second, d_pre_bf).astype(BF16)
    d_hidden_ln, gain_b_grad, shift_b_grad = norm_backward(d_second, normed_b, inv_b, gain_b)
    d_hidden = upstream + d_hidden_ln
    hidden_bf = d_hidden.astype(BF16)
    d_attended = dot(w_out, hidden_bf, 1, 1).astype(BF16)
    g_out = half_grad(later, attended.T, hidden_bf)
    d_joined = attention_backward(attn_saved, d_attended)
    _, cols, rows = d_joined.shape
    flat = d_joined.reshape(3 * cols, rows)
    d_first = tp_sum(dot(flat, w_qkv, 0, 1))
    g_qkv = half_grad(later, first, flat.T)
    d_in_ln, gain_a_grad, shift_a_grad = norm_backward(d_first, normed_a, inv_a, gain_a)
    bias_grads = jnp.sum(d_joined.astype(F32), axis=2)
    small = jnp.concatenate(
        [
            bias_grads[0],
            bias_grads[2],
            jnp.sum(d_hidden, axis=0),
            jnp.sum(d_pre, axis=0),
            jnp.sum(upstream, axis=0),
            gain_a_grad,
            gain_b_grad,
            shift_a_grad,
            shift_b_grad,
        ]
    )
    return d_hidden + d_in_ln, (g_proj, g_fc), (g_out, g_qkv), small


def body(
    layer_input, cotangent, w_qkv, b_qv, w_out, b_out, w_fc, b_fc, w_proj, b_proj, ln_gain, ln_bias
):
    later = lax.axis_index("section") == 1
    width = layer_input.shape[2]
    cols = w_out.shape[1]

    def both_layers(own):
        other = swap(own)
        return jnp.where(later, other, own), jnp.where(later, own, other)

    vec_parts = [
        b_qv[0, 0], b_qv[0, 1], b_out[0], b_fc[0], b_proj[0],
        ln_gain[0, 0], ln_gain[0, 1], ln_bias[0, 0], ln_bias[0, 1],
    ]
    bounds = []
    for part in vec_parts:
        bounds.append((bounds[-1] if bounds else 0) + part.shape[0])
    vec_pair = both_layers(jnp.concatenate([part.astype(F32) for part in vec_parts]))
    vecs = [jnp.split(vec, bounds[:-1]) for vec in vec_pair]
    mats = [
        both_layers(mat)
        for mat in (w_qkv[0].reshape(width, 3 * cols), w_out[0], w_fc[0], w_proj[0])
    ]
    weights = [[pair[layer] for pair in mats] for layer in range(2)]

    start = jnp.where(later, layer_input[1], layer_input[0])
    act_0, saved_0 = layer_forward(start, weights[0], vecs[0])
    act_1, saved_1 = layer_forward(act_0, weights[1], vecs[1])
    got_act = swap(jnp.where(later, act_0, act_1))
    activations = jnp.stack([jnp.where(later, got_act, act_0), jnp.where(later, act_1, got_act)])

    upstream = jnp.where(later, cotangent[1], cotangent[0]).astype(F32)
    d_1, ffn_1, attn_1, small_1 = layer_backward(upstream, saved_1, weights[1], vecs[1], later)
    ffn_1 = [lax.psum(half, "ctx") for half in ffn_1]
    attn_1 = attn_sums(*attn_1)
    d_0, ffn_0, attn_0, small_0 = layer_backward(d_1, saved_0, weights[0], vecs[0], later)
    small = jnp.where(later, small_1, small_0) + swap(jnp.where(later, small_0, small_1))
    g_proj_0, g_fc_0 = ffn_0
    span = g_fc_0.shape[1]
    small_rows = -(-small.shape[0] // span)
    small_rows += -small_rows % 16
    small_pad = jnp.pad(small.astype(BF16), (0, small_rows * span - small.shape[0]))
    last = [g_proj_0, jnp.concatenate([g_fc_0, small_pad.reshape(small_rows, span)])]
    last, ffn_1, attn_0 = lax.optimization_barrier((last, ffn_1, attn_0))
    attn_0 = attn_sums(*attn_0)
    g_proj_0, packed = [lax.psum(half, "ctx") for half in last]
    small = packed[-small_rows:].astype(F32).reshape(-1)[: small.shape[0]]
    sums_1 = ffn_1 + attn_1
    sums_0 = [g_proj_0, packed[:-small_rows]] + attn_0
    up_1 = [lax.ppermute(half, "section", [(0, 1)]) for half in sums_1]
    down_0 = [lax.ppermute(half, "section", [(1, 0)]) for half in sums_0]

    got_grad = swap(jnp.where(later, d_0, d_1).astype(BF16)).astype(F32)
    input_grads = jnp.stack([jnp.where(later, got_grad, d_0), jnp.where(later, d_1, got_grad)])

    def joined_halves(own_0, own_1, got_0, got_1):
        low = jnp.where(later, got_1, own_0)
        high = jnp.where(later, own_1, got_0)
        return jnp.concatenate([low, high]).astype(F32)

    g_proj, g_fc, g_out, g_qkv = [
        joined_halves(*group) for group in zip(sums_0, sums_1, down_0, up_1)
    ]
    small = jnp.split(small, bounds[:-1])
    return (
        activations[None],
        input_grads[None],
        g_qkv.reshape(1, width, 3, cols),
        jnp.stack([small[0], small[1]])[None],
        g_out[None],
        small[2][None],
        g_fc[None],
        small[3][None],
        g_proj[None],
        small[4][None],
        jnp.stack([small[5], small[6]])[None],
        jnp.stack([small[7], small[8]])[None],
    )


def solution(mesh):
    placed = (
        P(None, "ctx", None),
        P(None, "ctx", None),
        P("section", None, None, "tp"),
        P("section", None, "tp"),
        P("section", "tp", None),
        P("section", None),
        P("section", None, "tp"),
        P("section", "tp"),
        P("section", "tp", None),
        P("section", None),
        P("section", None, None),
        P("section", None, None),
    )
    return jax.shard_map(
        body,
        mesh=mesh,
        in_specs=placed,
        out_specs=(
            P("section", None, "ctx", None),
            P("section", None, "ctx", None),
            P("section", None, None, "tp"),
            P("section", None, "tp"),
            P("section", "tp", None),
            P("section", None),
            P("section", None, "tp"),
            P("section", "tp"),
            P("section", "tp", None),
            P("section", None),
            P("section", None, None),
            P("section", None, None),
        ),
        check_vma=False,
    )
```
